32 devices in a mesh: ex: 8 (over z, x), tp: 4 (over y, core).
Axes of the slice: x: 2, y: 2, z: 4, core: 2. Of those that a mesh axis runs over, the one named last changes fastest.
Arguments:
- acts: bfloat16 [8192, 4096], P('ex', 'tp'), may hold values from -6 to 6
- out_grads: bfloat16 [8192, 14336], P('ex', 'tp'), may hold values from -6 to 6
- basis_in: bfloat16 [4096, 128], P('tp'), may hold values from -0.09375 to 0.09375
- basis_out: bfloat16 [14336, 128], P('tp'), may hold values from -0.046875 to 0.046875
- eigen: float32 [128, 128], replicated, may hold values from 0.05 to 5
- query_grads: bfloat16 [256, 16384], P('ex'), may hold values from -0.046875 to 0.046875
- candidates: int32 [64, 4], P(('ex', 'tp')), may hold values from 0 to 7, as said below
- counts: int32 [64], P(('ex', 'tp')), may hold values from 2 to 4
- owner_map: int32 [8], replicated, may hold values from 0 to 7, each once
Outputs:
- scores: float32 [64, 4, 32], P(('ex', 'tp'))
The draws below stay inside these ranges and needn't reach their ends.
Inputs may be any that keep to these rules, and one draw needn't show every extreme that they name: `candidates`: each row holds 4 different query blocks; one block, the same for every row of a draw, is the first entry of every row; entries at or after counts[n] are not used.
All inputs are finite; a program needn't handle non-finite values.
Results may differ from the reference program's by a relative error of at most 0.0029.
Values may be sent and summed in bfloat16 or wider, within the bound.
A program may use at most 128 MiB of HBM per device.

```python
import math
import jax
import jax.numpy as jnp
from jax import lax

D = 4096
FF = 14336
KA = 128
KG = 128
SEQ = 128
QB = 32
C = 4
TOKENS = 8192
TRAIN = 64
KK = 16384
QUERIES = 256
N_EX = 8


def draw_candidates(key, part):
    key_noise = jax.random.fold_in(key, 11)
    key_pop = jax.random.fold_in(key, 12)
    key_hot = jax.random.fold_in(key, 13)
    noise = jax.random.randint(key_noise, (TRAIN, N_EX), 0, 1000)
    popular = jax.random.randint(key_pop, (N_EX,), 0, 4) * 500
    hot = jax.random.randint(key_hot, (), 0, N_EX)
    blocks = jnp.arange(N_EX, dtype=jnp.int32)
    score = noise + popular[None, :] + jnp.where(blocks == hot, 1000000, 0)[None, :]
    score = score * N_EX + blocks[None, :]
    values, picked = lax.top_k(score, C)
    return picked.astype(jnp.int32)


def draw_counts(key, part):
    key_len = jax.random.fold_in(key, 21)
    lengths = jax.random.randint(key_len, (TRAIN,), C // 2, C + 1)
    lengths = lengths.at[0].set(C)
    lengths = lengths.at[TRAIN - 1].set(C // 2)
    return lengths.astype(jnp.int32)


def levels(rng, extent, split, smallest, largest):
    def one(axis_at, blocks):
        draws = jax.random.uniform(jax.random.fold_in(jax.random.fold_in(rng, 6), axis_at), (blocks,), jnp.float32, smallest / len(split), largest / len(split))
        return jnp.repeat(jnp.exp(draws), extent[axis_at] // blocks).reshape((-1,) + (1,) * (len(extent) - axis_at - 1))

    loudness = one(*split[0])
    for cut in split[1:]:
        loudness = loudness * one(*cut)
    return loudness


def bell_draw(rng, extent, deviation, reach, shards=(), kind=jnp.bfloat16):
    gain = levels(rng, extent, shards, -0.22, 0.18) if shards else 1.0
    array = jax.random.normal(rng, extent, jnp.float32) * deviation * gain
    return jnp.minimum(jnp.maximum(array, -reach), reach).astype(kind)


def setup_inputs(seed: int = 0) -> dict:
    seeds = jax.random.split(jax.random.key(seed), 10)
    return {
        "acts": bell_draw(seeds[0], (TOKENS, D), 1.0, 6.0, ((0, 8), (1, 4))),
        "out_grads": bell_draw(seeds[1], (TOKENS, FF), 1.0, 6.0, ((0, 8), (1, 4))),
        "basis_in": bell_draw(seeds[2], (D, KA), D ** -0.5, 0.09375, ((0, 4),)),
        "basis_out": bell_draw(seeds[3], (FF, KG), FF ** -0.5, 0.046875, ((0, 4),)),
        "eigen": jnp.clip(jnp.exp(jax.random.uniform(seeds[4], (KG, KA), jnp.float32, math.log(0.05), math.log(5.0))), 0.05, 5.0),
        "query_grads": bell_draw(seeds[5], (QUERIES, KK), KK ** -0.5, 0.046875, ((0, 8),)),
        "candidates": draw_candidates(jax.random.fold_in(seeds[9], 71), 0),
        "counts": draw_counts(jax.random.fold_in(seeds[9], 71), 0),
        "owner_map": jax.random.permutation(seeds[8], N_EX).astype(jnp.int32),
    }


DAMP = 0.05


def reference(acts, out_grads, basis_in, basis_out, eigen, query_grads, candidates, counts, owner_map):
    proj_in = jnp.dot(acts, basis_in, preferred_element_type=jnp.float32)
    proj_out = jnp.dot(out_grads, basis_out, preferred_element_type=jnp.float32)
    seqs = proj_in.shape[0] // SEQ
    pin = proj_in.reshape(seqs, SEQ, KA)
    pout = proj_out.reshape(seqs, SEQ, KG)
    grad = jnp.einsum("nsg,nsa->nga", pout, pin, precision=lax.Precision.HIGHEST) / SEQ
    rows = (grad / (eigen + DAMP)).astype(jnp.bfloat16).reshape(seqs, KA * KG)
    blocks = query_grads.reshape(N_EX, QB, KA * KG)
    slots = jnp.arange(C, dtype=jnp.int32)

    def score_one(item):
        row, cand, count = item
        owners = owner_map[cand]
        chosen = blocks[owners].astype(jnp.float32)
        values = jnp.einsum("k,cqk->cq", row.astype(jnp.float32), chosen, precision=lax.Precision.HIGHEST)
        return jnp.where((slots < count)[:, None], values, jnp.float32(0.0))

    return lax.map(score_one, (rows, candidates, counts))
```

```python
import jax
import jax.numpy as jnp
from jax import lax
from jax.sharding import PartitionSpec as P

KA = 128
KG = 128
SEQ = 128


DAMP = 0.05


def shards(acts, out_grads, basis_in, basis_out, eigen, query_grads, candidates, counts, owner_map):
    owners_total = lax.axis_size("ex")
    part_in = jnp.dot(acts, basis_in, preferred_element_type=jnp.float32)
    part_out = jnp.dot(out_grads, basis_out, preferred_element_type=jnp.float32)
    both = lax.psum_scatter(
        jnp.concatenate([part_in, part_out], axis=1), "tp", scatter_dimension=0, tiled=True
    )
    proj_in, proj_out = both[:, :KA], both[:, KA:]
    examples = counts.shape[0]
    slot_total = candidates.shape[1]
    pin = proj_in.reshape(examples, SEQ, KA)
    pout = proj_out.reshape(examples, SEQ, KG)
    grad = jnp.einsum("nsg,nsa->nga", pout, pin, precision=lax.Precision.HIGHEST) / SEQ
    rows = (grad / (eigen + DAMP)).astype(jnp.bfloat16).reshape(examples, KA * KG)
    block_ids = jnp.arange(owners_total, dtype=jnp.int32)
    owner_of = jnp.sum(
        jnp.where(candidates[:, :, None] == block_ids[None, None, :], owner_map[None, None, :], 0),
        axis=2,
    )
    valid = jnp.arange(slot_total, dtype=jnp.int32)[None, :] < counts[:, None]
    target = (owner_of[:, :, None] == block_ids[None, None, :]) & valid[:, :, None]
    values = jnp.einsum(
        "oik,qk->oiq",
        lax.all_gather(rows, "ex", axis=0),
        query_grads,
        preferred_element_type=jnp.float32,
    )
    returned = lax.all_to_all(values, "ex", split_axis=0, concat_axis=0, tiled=True)
    return jnp.einsum(
        "jco,ojq->jcq", target.astype(jnp.float32), returned, precision=lax.Precision.HIGHEST
    )


def solution(mesh):
    in_specs = (
        P("ex", "tp"),
        P("ex", "tp"),
        P("tp", None),
        P("tp", None),
        P(),
        P("ex", None),
        P(("ex", "tp"), None),
        P(("ex", "tp")),
        P(),
    )
    out_specs = P(("ex", "tp"), None, None)
    return jax.shard_map(shards, mesh=mesh, in_specs=in_specs, out_specs=out_specs, check_vma=False)
```

```python
import functools

import jax
import jax.numpy as jnp
from jax import lax
from jax.experimental import pallas as pl
from jax.experimental.pallas import tpu as pltpu
from jax.sharding import PartitionSpec as P

MESH = pl.DeviceIdType.MESH
KA = 128
KG = 128
SEQ = 128
DAMP = 0.05


def kernel(
    owners,
    examples,
    acts_ref,
    grads_ref,
    bin_ref,
    bout_ref,
    eigen_ref,
    query_ref,
    out_ref,
    acts_v,
    grads_v,
    bin_v,
    bout_v,
    eigen_v,
    query_v,
    part,
    landed,
    total,
    ratio,
    flat,
    rows,
    gathered,
    wide,
    scores,
    load_sem,
    tp_send,
    tp_recv,
    row_send,
    row_recv,
    val_send,
    val_recv,
):
    ex = lax.axis_index("ex")
    tp = lax.axis_index("tp")
    y, c = tp // 2, tp % 2
    near = 2 * y + (1 - c)
    far = 2 * (1 - y) + c
    tokens = examples * SEQ
    queries = query_ref.shape[0]

    barrier = pltpu.get_barrier_semaphore()
    for peer in (near, far):
        pl.semaphore_signal(barrier, inc=1, device_id=(ex, peer), device_id_type=MESH)
    for k in range(1, owners):
        pl.semaphore_signal(
            barrier, inc=1, device_id=((ex + k) % owners, tp), device_id_type=MESH
        )

    chunks = (2 * (1 - y) + (1 - c), far, near, tp)
    load_b = (
        pltpu.make_async_copy(bin_ref, bin_v, load_sem.at[0]),
        pltpu.make_async_copy(bout_ref, bout_v, load_sem.at[1]),
    )
    load_e = pltpu.make_async_copy(eigen_ref, eigen_v, load_sem.at[2])
    load_q = pltpu.make_async_copy(query_ref, query_v, load_sem.at[3])
    loads = []
    for i, d in enumerate(chunks):
        span = pl.ds(pl.multiple_of(d * tokens, tokens), tokens)
        loads.append(
            (
                pltpu.make_async_copy(acts_ref.at[span], acts_v.at[i], load_sem.at[4 + 2 * i]),
                pltpu.make_async_copy(grads_ref.at[span], grads_v.at[i], load_sem.at[5 + 2 * i]),
            )
        )
    for copy in load_b:
        copy.start()
    for pair in loads:
        for copy in pair:
            copy.start()
    load_e.start()
    load_q.start()
    for copy in load_b:
        copy.wait()

    def project(i):
        for copy in loads[i]:
            copy.wait()
        part[i, :, :KA] = jnp.dot(acts_v[i], bin_v[...], preferred_element_type=jnp.float32)
        part[i, :, KA:] = jnp.dot(grads_v[i], bout_v[...], preferred_element_type=jnp.float32)

    def send(i, slot, peer):
        return pltpu.make_async_remote_copy(
            src_ref=part.at[i],
            dst_ref=landed.at[slot],
            send_sem=tp_send.at[slot],
            recv_sem=tp_recv.at[slot],
            device_id=(ex, peer),
            device_id_type=MESH,
        )

    project(0)
    pl.semaphore_wait(barrier, 2 + owners - 1)
    first = send(0, 0, near)
    first.start()
    project(1)
    first.wait_recv()
    part[1] += landed[0]
    across = send(1, 1, far)
    across.start()
    project(2)
    second = send(2, 2, near)
    second.start()
    project(3)
    second.wait_recv()
    total[...] = part[3] + landed[2]
    load_e.wait()
    scale = eigen_v[...] + DAMP
    across.wait_recv()
    total[...] += landed[1]

    for n in range(examples):
        span = slice(n * SEQ, (n + 1) * SEQ)
        grad = lax.dot_general(
            total[span, KA:],
            total[span, :KA],
            (((0,), (0,)), ((), ())),
            precision=lax.Precision.HIGHEST,
            preferred_element_type=jnp.float32,
        )
        ratio[span] = (grad / SEQ) / scale
    for g in range(KG):
        for n in range(examples):
            flat[n : n + 1, g * KA : (g + 1) * KA] = ratio[n * SEQ + g : n * SEQ + g + 1, :]
    rows[...] = flat[...].astype(jnp.bfloat16)
    row_copies = [None]
    for k in range(1, owners):
        copy = pltpu.make_async_remote_copy(
            src_ref=rows,
            dst_ref=gathered.at[k],
            send_sem=row_send.at[k],
            recv_sem=row_recv.at[k],
            device_id=((ex + k) % owners, tp),
            device_id_type=MESH,
        )
        copy.start()
        row_copies.append(copy)
    wide[0:examples, :] = rows[...].astype(jnp.float32)
    load_q.wait()
    for k in range(1, owners):
        row_copies[k].wait_recv()
        wide[k * examples : (k + 1) * examples, :] = gathered[k].astype(jnp.float32)
    values = lax.dot_general(
        wide[...].astype(jnp.bfloat16),
        query_v[...],
        (((1,), (1,)), ((), ())),
        preferred_element_type=jnp.float32,
    )
    scores[...] = jnp.zeros_like(scores)
    for k in range(owners):
        scores[k, :, :queries] = values[k * examples : (k + 1) * examples, :]
    out_ref[0] = scores[0]
    val_copies = []
    for k in range(1, owners):
        copy = pltpu.make_async_remote_copy(
            src_ref=scores.at[k],
            dst_ref=out_ref.at[k],
            send_sem=val_send.at[k],
            recv_sem=val_recv.at[k],
            device_id=((ex - k + owners) % owners, tp),
            device_id_type=MESH,
        )
        copy.start()
        val_copies.append(copy)
    for k in range(1, owners):
        row_copies[k].wait_send()
    for copy in (first, across, second):
        copy.wait_send()
    for copy in val_copies:
        copy.wait()


def shards(acts, out_grads, basis_in, basis_out, eigen, query_grads, candidates, counts, owner_map):
    owners = lax.axis_size("ex")
    assert lax.axis_size("tp") == 4
    examples, slot_total = candidates.shape
    tokens = examples * SEQ
    queries, kk = query_grads.shape
    vmem = pltpu.VMEM
    dma = pltpu.SemaphoreType.DMA
    returned = pl.pallas_call(
        functools.partial(kernel, owners, examples),
        out_shape=jax.ShapeDtypeStruct((owners, examples, 128), jnp.float32),
        in_specs=[pl.BlockSpec(memory_space=pl.ANY)] * 6,
        out_specs=pl.BlockSpec(memory_space=pltpu.VMEM),
        scratch_shapes=[
            vmem((4, tokens, acts.shape[1]), jnp.bfloat16),
            vmem((4, tokens, out_grads.shape[1]), jnp.bfloat16),
            vmem(basis_in.shape, jnp.bfloat16),
            vmem(basis_out.shape, jnp.bfloat16),
            vmem(eigen.shape, jnp.float32),
            vmem(query_grads.shape, jnp.bfloat16),
            vmem((4, tokens, KA + KG), jnp.float32),
            vmem((3, tokens, KA + KG), jnp.float32),
            vmem((tokens, KA + KG), jnp.float32),
            vmem((tokens, KA), jnp.float32),
            vmem((examples, kk), jnp.float32),
            vmem((examples, kk), jnp.bfloat16),
            vmem((owners, examples, kk), jnp.bfloat16),
            vmem((owners * examples, kk), jnp.float32),
            vmem((owners, examples, 128), jnp.float32),
            dma((12,)),
            dma((3,)),
            dma((3,)),
            dma((owners,)),
            dma((owners,)),
            dma((owners,)),
            dma((owners,)),
        ],
        compiler_params=pltpu.CompilerParams(
            collective_id=0, has_side_effects=True, vmem_limit_bytes=60 << 20
        ),
    )(acts, out_grads, basis_in, basis_out, eigen, query_grads)
    block_ids = jnp.arange(owners, dtype=jnp.int32)
    owner_of = jnp.sum(
        jnp.where(candidates[:, :, None] == block_ids[None, None, :], owner_map[None, None, :], 0),
        axis=2,
    )
    valid = jnp.arange(slot_total, dtype=jnp.int32)[None, :] < counts[:, None]
    holder = (lax.axis_index("ex") + block_ids) % owners
    target = (owner_of[:, :, None] == holder[None, None, :]) & valid[:, :, None]
    values = returned[:, :, :queries].transpose(1, 0, 2)
    return jnp.sum(jnp.where(target[:, :, :, None], values[:, None, :, :], 0.0), axis=2)


def solution(mesh):
    in_specs = (
        P("ex", "tp"),
        P("ex", "tp"),
        P("tp", None),
        P("tp", None),
        P(),
        P("ex", None),
        P(("ex", "tp"), None),
        P(("ex", "tp")),
        P(),
    )
    out_specs = P(("ex", "tp"), None, None)
    return jax.shard_map(shards, mesh=mesh, in_specs=in_specs, out_specs=out_specs, check_vma=False)
```

```python
import functools

import jax
import jax.numpy as jnp
from jax import lax
from jax.experimental import pallas as pl
from jax.experimental.pallas import tpu as pltpu
from jax.sharding import PartitionSpec as P

MESH = pl.DeviceIdType.MESH
KA = 128
KG = 128
SEQ = 128
DAMP = 0.05


def kernel(
    owners,
    examples,
    acts_ref,
    grads_ref,
    bin_ref,
    bout_ref,
    eigen_ref,
    query_ref,
    out_ref,
    acts_v,
    grads_v,
    bin_v,
    bout_v,
    eigen_v,
    query_v,
    part,
    landed,
    total,
    ratio,
    flat,
    rows,
    gathered,
    wide,
    scores,
    returned,
    load_sem,
    tp_send,
    tp_recv,
    query_send,
    query_recv,
    row_send,
    row_recv,
    val_send,
    val_recv,
):
    ex = lax.axis_index("ex")
    tp = lax.axis_index("tp")
    hi, lo = ex // 4, ex % 4
    groups = owners // 4
    y, c = tp // 2, tp % 2
    near = 2 * y + (1 - c)
    far = 2 * (1 - y) + c
    tokens = examples * SEQ
    queries = query_ref.shape[0]
    quarter = query_ref.shape[1] // 4
    slots = [(h, j) for h in range(groups) for j in range(4)]

    def row_peer(h, j):
        return (((hi + h) % groups) * 4 + lo, (tp + j) % 4)

    def row_source(h, j):
        return (((hi - h + groups) % groups) * 4 + lo, (tp - j + 4) % 4)

    def query_peer(m):
        return (hi * 4 + (lo + m) % 4, tp)

    barrier = pltpu.get_barrier_semaphore()
    for h, j in slots[1:]:
        pl.semaphore_signal(barrier, inc=1, device_id=row_peer(h, j), device_id_type=MESH)
    for m in range(1, 4):
        pl.semaphore_signal(barrier, inc=1, device_id=query_peer(m), device_id_type=MESH)

    chunks = (2 * (1 - y) + (1 - c), far, near, tp)
    load_b = (
        pltpu.make_async_copy(bin_ref, bin_v, load_sem.at[0]),
        pltpu.make_async_copy(bout_ref, bout_v, load_sem.at[1]),
    )
    load_e = pltpu.make_async_copy(eigen_ref, eigen_v, load_sem.at[2])
    mine = query_ref.at[:, pl.ds(pl.multiple_of(tp * quarter, quarter), quarter)]
    load_q = pltpu.make_async_copy(mine, query_v.at[pl.ds(0, queries)], load_sem.at[3])
    loads = []
    for i, d in enumerate(chunks):
        span = pl.ds(pl.multiple_of(d * tokens, tokens), tokens)
        loads.append(
            (
                pltpu.make_async_copy(acts_ref.at[span], acts_v.at[i], load_sem.at[4 + 2 * i]),
                pltpu.make_async_copy(grads_ref.at[span], grads_v.at[i], load_sem.at[5 + 2 * i]),
            )
        )
    for copy in load_b:
        copy.start()
    for pair in loads:
        for copy in pair:
            copy.start()
    load_e.start()
    load_q.start()
    for copy in load_b:
        copy.wait()

    def project(i):
        for copy in loads[i]:
            copy.wait()
        part[i, :, :KA] = jnp.dot(acts_v[i], bin_v[...], preferred_element_type=jnp.float32)
        part[i, :, KA:] = jnp.dot(grads_v[i], bout_v[...], preferred_element_type=jnp.float32)

    def send(i, slot, peer):
        return pltpu.make_async_remote_copy(
            src_ref=part.at[i],
            dst_ref=landed.at[slot],
            send_sem=tp_send.at[slot],
            recv_sem=tp_recv.at[slot],
            device_id=(ex, peer),
            device_id_type=MESH,
        )

    project(0)
    pl.semaphore_wait(barrier, len(slots) - 1 + 3)
    first = send(0, 0, near)
    first.start()
    query_copies = []
    for m in range(1, 4):
        copy = pltpu.make_async_remote_copy(
            src_ref=mine,
            dst_ref=query_v.at[pl.ds(m * queries, queries)],
            send_sem=query_send.at[m],
            recv_sem=query_recv.at[m],
            device_id=query_peer(m),
            device_id_type=MESH,
        )
        copy.start()
        query_copies.append(copy)
    project(1)
    first.wait_recv()
    part[1] += landed[0]
    across = send(1, 1, far)
    across.start()
    project(2)
    second = send(2, 2, near)
    second.start()
    project(3)
    second.wait_recv()
    total[...] = part[3] + landed[2]
    load_e.wait()
    scale = eigen_v[...] + DAMP
    across.wait_recv()
    total[...] += landed[1]

    for n in range(examples):
        span = slice(n * SEQ, (n + 1) * SEQ)
        grad = lax.dot_general(
            total[span, KA:],
            total[span, :KA],
            (((0,), (0,)), ((), ())),
            precision=lax.Precision.HIGHEST,
            preferred_element_type=jnp.float32,
        )
        ratio[span] = (grad / SEQ) / scale
    for g in range(KG):
        at = (g * KA) % quarter
        for n in range(examples):
            flat[g * KA // quarter, n : n + 1, at : at + KA] = ratio[n * SEQ + g : n * SEQ + g + 1, :]
    rows[...] = flat[...].astype(jnp.bfloat16)
    row_copies = []
    for s, (h, j) in enumerate(slots):
        if s == 0:
            continue
        copy = pltpu.make_async_remote_copy(
            src_ref=rows.at[(tp + j) % 4],
            dst_ref=gathered.at[s],
            send_sem=row_send.at[s],
            recv_sem=row_recv.at[s],
            device_id=row_peer(h, j),
            device_id_type=MESH,
        )
        copy.start()
        row_copies.append(copy)
    wide[0:examples, :] = rows[tp].astype(jnp.float32)
    load_q.wait()
    for copy in query_copies:
        copy.wait_recv()
    for s in range(1, len(slots)):
        row_copies[s - 1].wait_recv()
        wide[s * examples : (s + 1) * examples, :] = gathered[s].astype(jnp.float32)
    values = lax.dot_general(
        wide[...].astype(jnp.bfloat16),
        query_v[...],
        (((1,), (1,)), ((), ())),
        preferred_element_type=jnp.float32,
    )
    for s in range(len(slots)):
        scores[s] = values[s * examples : (s + 1) * examples, :]
    val_copies = []
    for s, (h, j) in enumerate(slots):
        if s == 0:
            continue
        copy = pltpu.make_async_remote_copy(
            src_ref=scores.at[s],
            dst_ref=returned.at[s],
            send_sem=val_send.at[s],
            recv_sem=val_recv.at[s],
            device_id=row_source(h, j),
            device_id_type=MESH,
        )
        copy.start()
        val_copies.append(copy)
    for copy in (first, across, second, *query_copies, *row_copies):
        copy.wait_send()
    for copy in val_copies:
        copy.wait_recv()
    for h in range(groups):
        own = scores[0] if h == 0 else returned[4 * h]
        out_ref[h] = (own + returned[4 * h + 1]) + (returned[4 * h + 2] + returned[4 * h + 3])
    for copy in val_copies:
        copy.wait_send()


def shards(acts, out_grads, basis_in, basis_out, eigen, query_grads, candidates, counts, owner_map):
    owners = lax.axis_size("ex")
    assert lax.axis_size("tp") == 4 and owners % 4 == 0
    groups, quarter = owners // 4, query_grads.shape[1] // 4
    examples, slot_total = candidates.shape
    tokens = examples * SEQ
    queries = query_grads.shape[0]
    vmem = pltpu.VMEM
    dma = pltpu.SemaphoreType.DMA
    returned = pl.pallas_call(
        functools.partial(kernel, owners, examples),
        out_shape=jax.ShapeDtypeStruct((groups, examples, 4 * queries), jnp.float32),
        in_specs=[pl.BlockSpec(memory_space=pl.ANY)] * 6,
        out_specs=pl.BlockSpec(memory_space=pltpu.VMEM),
        scratch_shapes=[
            vmem((4, tokens, acts.shape[1]), jnp.bfloat16),
            vmem((4, tokens, out_grads.shape[1]), jnp.bfloat16),
            vmem(basis_in.shape, jnp.bfloat16),
            vmem(basis_out.shape, jnp.bfloat16),
            vmem(eigen.shape, jnp.float32),
            vmem((4 * queries, quarter), jnp.bfloat16),
            vmem((4, tokens, KA + KG), jnp.float32),
            vmem((3, tokens, KA + KG), jnp.float32),
            vmem((tokens, KA + KG), jnp.float32),
            vmem((tokens, KA), jnp.float32),
            vmem((4, examples, quarter), jnp.float32),
            vmem((4, examples, quarter), jnp.bfloat16),
            vmem((owners, examples, quarter), jnp.bfloat16),
            vmem((owners * examples, quarter), jnp.float32),
            vmem((owners, examples, 4 * queries), jnp.float32),
            vmem((owners, examples, 4 * queries), jnp.float32),
            dma((12,)),
            dma((3,)),
            dma((3,)),
            dma((4,)),
            dma((4,)),
            dma((owners,)),
            dma((owners,)),
            dma((owners,)),
            dma((owners,)),
        ],
        compiler_params=pltpu.CompilerParams(
            collective_id=0, has_side_effects=True, vmem_limit_bytes=60 << 20
        ),
    )(acts, out_grads, basis_in, basis_out, eigen, query_grads)
    block_ids = jnp.arange(owners, dtype=jnp.int32)
    owner_of = jnp.sum(
        jnp.where(candidates[:, :, None] == block_ids[None, None, :], owner_map[None, None, :], 0),
        axis=2,
    )
    valid = jnp.arange(slot_total, dtype=jnp.int32)[None, :] < counts[:, None]
    ex = lax.axis_index("ex")
    holder = ((ex // 4 + jnp.arange(groups)[:, None]) % groups) * 4 + (ex + jnp.arange(4, 0, -1)) % 4
    target = (owner_of[:, :, None] == holder.reshape(owners)) & valid[:, :, None]
    values = returned.reshape(groups, examples, 4, queries).transpose(1, 0, 2, 3)
    values = values.reshape(examples, 1, owners, queries)
    return jnp.sum(jnp.where(target[:, :, :, None], values, 0.0), axis=2)


def solution(mesh):
    in_specs = (
        P("ex", "tp"),
        P("ex", "tp"),
        P("tp", None),
        P("tp", None),
        P(),
        P("ex", None),
        P(("ex", "tp"), None),
        P(("ex", "tp")),
        P(),
    )
    out_specs = P(("ex", "tp"), None, None)
    return jax.shard_map(shards, mesh=mesh, in_specs=in_specs, out_specs=out_specs, check_vma=False)
```

```python
import functools

import jax
import jax.numpy as jnp
from jax import lax
from jax.experimental import pallas as pl
from jax.experimental.pallas import tpu as pltpu
from jax.sharding import PartitionSpec as P

MESH = pl.DeviceIdType.MESH
KA = 128
KG = 128
SEQ = 128
DAMP = 0.05


def kernel(
    owners,
    examples,
    acts_ref,
    grads_ref,
    bin_ref,
    bout_ref,
    eigen_ref,
    query_ref,
    out_ref,
    acts_v,
    grads_v,
    bin_v,
    bout_v,
    eigen_v,
    query_v,
    part,
    landed,
    total,
    ratio,
    flat,
    rows,
    gathered,
    wide,
    scores,
    returned,
    load_sem,
    tp_send,
    tp_recv,
    query_send,
    query_recv,
    row_send,
    row_recv,
    val_send,
    val_recv,
):
    ex = lax.axis_index("ex")
    tp = lax.axis_index("tp")
    hi, lo = ex // 4, ex % 4
    groups = owners // 4
    y, c = tp // 2, tp % 2
    near = 2 * y + (1 - c)
    far = 2 * (1 - y) + c
    tokens = examples * SEQ
    queries = query_ref.shape[0]
    quarter = query_ref.shape[1] // 4
    slots = [(h, j) for h in range(groups) for j in range(4)]

    def row_peer(h, j):
        return (((hi + h) % groups) * 4 + lo, (tp + j) % 4)

    def row_source(h, j):
        return (((hi - h + groups) % groups) * 4 + lo, (tp - j + 4) % 4)

    side = (ex - lo + 2 * (lo // 2) + 1 - lo % 2, tp)
    over = (ex - lo + 2 * (1 - lo // 2) + lo % 2, tp)

    barrier = pltpu.get_barrier_semaphore()
    for h, j in slots[1:]:
        pl.semaphore_signal(barrier, inc=1, device_id=row_peer(h, j), device_id_type=MESH)
    for peer in (side, over):
        pl.semaphore_signal(barrier, inc=1, device_id=peer, device_id_type=MESH)

    chunks = (2 * (1 - y) + (1 - c), far, near, tp)
    load_b = (
        pltpu.make_async_copy(bin_ref, bin_v, load_sem.at[0]),
        pltpu.make_async_copy(bout_ref, bout_v, load_sem.at[1]),
    )
    load_e = pltpu.make_async_copy(eigen_ref, eigen_v, load_sem.at[2])
    mine = query_ref.at[:, pl.ds(pl.multiple_of(tp * quarter, quarter), quarter)]
    load_q = pltpu.make_async_copy(mine, query_v.at[pl.ds(0, queries)], load_sem.at[3])
    loads = []
    for i, d in enumerate(chunks):
        span = pl.ds(pl.multiple_of(d * tokens, tokens), tokens)
        loads.append(
            (
                pltpu.make_async_copy(acts_ref.at[span], acts_v.at[i], load_sem.at[4 + 2 * i]),
                pltpu.make_async_copy(grads_ref.at[span], grads_v.at[i], load_sem.at[5 + 2 * i]),
            )
        )
    for copy in load_b:
        copy.start()
    for pair in loads:
        for copy in pair:
            copy.start()
    load_e.start()
    load_q.start()
    pl.semaphore_wait(barrier, len(slots) - 1 + 2)

    def pass_query(i, src, row, count, peer):
        return pltpu.make_async_remote_copy(
            src_ref=src,
            dst_ref=query_v.at[pl.ds(row, count)],
            send_sem=query_send.at[i],
            recv_sem=query_recv.at[i],
            device_id=peer,
            device_id_type=MESH,
        )

    half = queries // 2
    query_copies = [
        pass_query(0, mine, queries, queries, side),
        pass_query(1, mine, 2 * queries, queries, over),
        pass_query(2, query_v.at[pl.ds(2 * queries, half)], 3 * queries, half, side),
        pass_query(
            3, query_v.at[pl.ds(queries + half, half)], 3 * queries + half, half, over
        ),
    ]
    for copy in query_copies[:2]:
        copy.start()
    for copy in load_b:
        copy.wait()

    def project(i, start, size):
        span = pl.ds(start, size)
        part[i, span, :KA] = jnp.dot(
            acts_v[i, span], bin_v[...], preferred_element_type=jnp.float32
        )
        part[i, span, KA:] = jnp.dot(
            grads_v[i, span], bout_v[...], preferred_element_type=jnp.float32
        )

    def arrive(i):
        for copy in loads[i]:
            copy.wait()

    def send(i, slot, start, size, sem, peer):
        return pltpu.make_async_remote_copy(
            src_ref=part.at[i, pl.ds(start, size)],
            dst_ref=landed.at[slot, pl.ds(start, size)],
            send_sem=tp_send.at[sem],
            recv_sem=tp_recv.at[sem],
            device_id=(ex, peer),
            device_id_type=MESH,
        )

    arrive(0)
    first = []
    for n in range(examples):
        project(0, n * SEQ, SEQ)
        copy = send(0, 0, n * SEQ, SEQ, n, near)
        copy.start()
        first.append(copy)
    arrive(1)
    across = []
    for n in range(examples):
        project(1, n * SEQ, SEQ)
        first[n].wait_recv()
        span = slice(n * SEQ, (n + 1) * SEQ)
        part[1, span] += landed[0, span]
        copy = send(1, 1, n * SEQ, SEQ, examples + n, far)
        copy.start()
        across.append(copy)
    arrive(2)
    project(2, 0, tokens)
    second = send(2, 2, 0, tokens, 2 * examples, near)
    second.start()
    arrive(3)
    project(3, 0, tokens)
    load_e.wait()
    scale = eigen_v[...] + DAMP
    second.wait_recv()
    total[...] = part[3] + landed[2]
    query_copies[1].wait_recv()
    query_copies[2].start()
    query_copies[0].wait_recv()
    query_copies[3].start()

    for n in range(examples):
        span = slice(n * SEQ, (n + 1) * SEQ)
        across[n].wait_recv()
        both = total[span] + landed[1, span]
        grad = lax.dot_general(
            both[:, KA:],
            both[:, :KA],
            (((0,), (0,)), ((), ())),
            precision=lax.Precision.HIGHEST,
            preferred_element_type=jnp.float32,
        )
        ratio[span] = (grad / SEQ) / scale
        for g in range(KG):
            at = (g * KA) % quarter
            flat[g * KA // quarter, n : n + 1, at : at + KA] = ratio[n * SEQ + g : n * SEQ + g + 1, :]
    rows[...] = flat[...].astype(jnp.bfloat16)
    row_copies = []
    for s, (h, j) in enumerate(slots):
        if s == 0:
            continue
        copy = pltpu.make_async_remote_copy(
            src_ref=rows.at[(tp + j) % 4],
            dst_ref=gathered.at[s],
            send_sem=row_send.at[s],
            recv_sem=row_recv.at[s],
            device_id=row_peer(h, j),
            device_id_type=MESH,
        )
        copy.start()
        row_copies.append(copy)
    wide[0:examples, :] = rows[tp].astype(jnp.float32)
    load_q.wait()
    for copy in query_copies[2:]:
        copy.wait_recv()
    for s in range(1, len(slots)):
        row_copies[s - 1].wait_recv()
        wide[s * examples : (s + 1) * examples, :] = gathered[s].astype(jnp.float32)
    values = lax.dot_general(
        wide[...].astype(jnp.bfloat16),
        query_v[...],
        (((1,), (1,)), ((), ())),
        preferred_element_type=jnp.float32,
    )
    for s in range(len(slots)):
        scores[s] = values[s * examples : (s + 1) * examples, :]
    val_copies = []
    for s, (h, j) in enumerate(slots):
        if s == 0:
            continue
        copy = pltpu.make_async_remote_copy(
            src_ref=scores.at[s],
            dst_ref=returned.at[s],
            send_sem=val_send.at[s],
            recv_sem=val_recv.at[s],
            device_id=row_source(h, j),
            device_id_type=MESH,
        )
        copy.start()
        val_copies.append(copy)
    for copy in (*first, *across, second, *query_copies, *row_copies):
        copy.wait_send()
    for copy in val_copies:
        copy.wait_recv()
    for h in range(groups):
        own = scores[0] if h == 0 else returned[4 * h]
        out_ref[h] = (own + returned[4 * h + 1]) + (returned[4 * h + 2] + returned[4 * h + 3])
    for copy in val_copies:
        copy.wait_send()


def shards(acts, out_grads, basis_in, basis_out, eigen, query_grads, candidates, counts, owner_map):
    owners = lax.axis_size("ex")
    assert lax.axis_size("tp") == 4 and owners % 4 == 0
    groups, quarter = owners // 4, query_grads.shape[1] // 4
    examples, slot_total = candidates.shape
    tokens = examples * SEQ
    queries = query_grads.shape[0]
    vmem = pltpu.VMEM
    dma = pltpu.SemaphoreType.DMA
    returned = pl.pallas_call(
        functools.partial(kernel, owners, examples),
        out_shape=jax.ShapeDtypeStruct((groups, examples, 4 * queries), jnp.float32),
        in_specs=[pl.BlockSpec(memory_space=pl.ANY)] * 6,
        out_specs=pl.BlockSpec(memory_space=pltpu.VMEM),
        scratch_shapes=[
            vmem((4, tokens, acts.shape[1]), jnp.bfloat16),
            vmem((4, tokens, out_grads.shape[1]), jnp.bfloat16),
            vmem(basis_in.shape, jnp.bfloat16),
            vmem(basis_out.shape, jnp.bfloat16),
            vmem(eigen.shape, jnp.float32),
            vmem((4 * queries, quarter), jnp.bfloat16),
            vmem((4, tokens, KA + KG), jnp.float32),
            vmem((3, tokens, KA + KG), jnp.float32),
            vmem((tokens, KA + KG), jnp.float32),
            vmem((tokens, KA), jnp.float32),
            vmem((4, examples, quarter), jnp.float32),
            vmem((4, examples, quarter), jnp.bfloat16),
            vmem((owners, examples, quarter), jnp.bfloat16),
            vmem((owners * examples, quarter), jnp.float32),
            vmem((owners, examples, 4 * queries), jnp.float32),
            vmem((owners, examples, 4 * queries), jnp.float32),
            dma((12,)),
            dma((2 * examples + 1,)),
            dma((2 * examples + 1,)),
            dma((4,)),
            dma((4,)),
            dma((owners,)),
            dma((owners,)),
            dma((owners,)),
            dma((owners,)),
        ],
        compiler_params=pltpu.CompilerParams(
            collective_id=0, has_side_effects=True, vmem_limit_bytes=60 << 20
        ),
    )(acts, out_grads, basis_in, basis_out, eigen, query_grads)
    block_ids = jnp.arange(owners, dtype=jnp.int32)
    owner_of = jnp.sum(
        jnp.where(candidates[:, :, None] == block_ids[None, None, :], owner_map[None, None, :], 0),
        axis=2,
    )
    valid = jnp.arange(slot_total, dtype=jnp.int32)[None, :] < counts[:, None]
    ex = lax.axis_index("ex")
    holder = ((ex // 4 + jnp.arange(groups)[:, None]) % groups) * 4 + ((ex % 4) ^ jnp.arange(4))
    target = (owner_of[:, :, None] == holder.reshape(owners)) & valid[:, :, None]
    values = returned.reshape(groups, examples, 4, queries).transpose(1, 0, 2, 3)
    values = values.reshape(examples, 1, owners, queries)
    return jnp.sum(jnp.where(target[:, :, :, None], values, 0.0), axis=2)


def solution(mesh):
    in_specs = (
        P("ex", "tp"),
        P("ex", "tp"),
        P("tp", None),
        P("tp", None),
        P(),
        P("ex", None),
        P(("ex", "tp"), None),
        P(("ex", "tp")),
        P(),
    )
    out_specs = P(("ex", "tp"), None, None)
    return jax.shard_map(shards, mesh=mesh, in_specs=in_specs, out_specs=out_specs, check_vma=False)
```

```python
import functools

import jax
import jax.numpy as jnp
from jax import lax
from jax.experimental import pallas as pl
from jax.experimental.pallas import tpu as pltpu
from jax.sharding import PartitionSpec as P

MESH = pl.DeviceIdType.MESH
KA = 128
KG = 128
SEQ = 128
DAMP = 0.05


def kernel(
    owners,
    examples,
    acts_ref,
    grads_ref,
    bin_ref,
    bout_ref,
    eigen_ref,
    query_ref,
    cand_in,
    count_in,
    map_in,
    out_ref,
    acts_v,
    grads_v,
    bin_v,
    bout_v,
    eigen_v,
    query_v,
    part,
    landed,
    total,
    ratio,
    flat,
    rows,
    gathered,
    wide,
    scores,
    returned,
    picked,
    cand_ref,
    count_ref,
    map_ref,
    load_sem,
    tp_send,
    tp_recv,
    query_send,
    query_recv,
    row_send,
    row_recv,
    val_send,
    val_recv,
):
    ex = lax.axis_index("ex")
    tp = lax.axis_index("tp")
    hi, lo = ex // 4, ex % 4
    groups = owners // 4
    y, c = tp // 2, tp % 2
    near = 2 * y + (1 - c)
    far = 2 * (1 - y) + c
    tokens = examples * SEQ
    queries = query_ref.shape[0]
    quarter = query_ref.shape[1] // 4
    slots = [(h, j) for h in range(groups) for j in range(4)]

    def row_peer(h, j):
        return (((hi + h) % groups) * 4 + lo, (tp + j) % 4)

    def row_source(h, j):
        return (((hi - h + groups) % groups) * 4 + lo, (tp - j + 4) % 4)

    side = (ex - lo + 2 * (lo // 2) + 1 - lo % 2, tp)
    over = (ex - lo + 2 * (1 - lo // 2) + lo % 2, tp)

    barrier = pltpu.get_barrier_semaphore()
    for h, j in slots[1:]:
        pl.semaphore_signal(barrier, inc=1, device_id=row_peer(h, j), device_id_type=MESH)
    for peer in (side, over):
        pl.semaphore_signal(barrier, inc=1, device_id=peer, device_id_type=MESH)

    chunks = (2 * (1 - y) + (1 - c), far, near, tp)
    load_b = (
        pltpu.make_async_copy(bin_ref, bin_v, load_sem.at[0]),
        pltpu.make_async_copy(bout_ref, bout_v, load_sem.at[1]),
    )
    load_e = pltpu.make_async_copy(eigen_ref, eigen_v, load_sem.at[2])
    mine = query_ref.at[:, pl.ds(pl.multiple_of(tp * quarter, quarter), quarter)]
    load_q = pltpu.make_async_copy(mine, query_v.at[pl.ds(0, queries)], load_sem.at[3])
    loads = []
    for i, d in enumerate(chunks):
        span = pl.ds(pl.multiple_of(d * tokens, tokens), tokens)
        loads.append(
            (
                pltpu.make_async_copy(acts_ref.at[span], acts_v.at[i], load_sem.at[4 + 2 * i]),
                pltpu.make_async_copy(grads_ref.at[span], grads_v.at[i], load_sem.at[5 + 2 * i]),
            )
        )
    for copy in load_b:
        copy.start()
    for pair in loads:
        for copy in pair:
            copy.start()
    load_e.start()
    tables = [
        pltpu.make_async_copy(src, dst, load_sem.at[12 + i])
        for i, (src, dst) in enumerate(
            ((cand_in, cand_ref), (count_in, count_ref), (map_in, map_ref))
        )
    ]
    for copy in tables:
        copy.start()
    load_q.start()
    pl.semaphore_wait(barrier, len(slots) - 1 + 2)

    def pass_query(i, src, row, count, peer):
        return pltpu.make_async_remote_copy(
            src_ref=src,
            dst_ref=query_v.at[pl.ds(row, count)],
            send_sem=query_send.at[i],
            recv_sem=query_recv.at[i],
            device_id=peer,
            device_id_type=MESH,
        )

    half = queries // 2
    query_copies = [
        pass_query(0, mine, queries, queries, side),
        pass_query(1, mine, 2 * queries, queries, over),
        pass_query(2, query_v.at[pl.ds(2 * queries, half)], 3 * queries, half, side),
        pass_query(
            3, query_v.at[pl.ds(queries + half, half)], 3 * queries + half, half, over
        ),
    ]
    for copy in query_copies[:2]:
        copy.start()
    for copy in load_b:
        copy.wait()

    def project(i, start, size):
        span = pl.ds(start, size)
        part[i, span, :KA] = jnp.dot(
            acts_v[i, span], bin_v[...], preferred_element_type=jnp.float32
        )
        part[i, span, KA:] = jnp.dot(
            grads_v[i, span], bout_v[...], preferred_element_type=jnp.float32
        )

    def arrive(i):
        for copy in loads[i]:
            copy.wait()

    def send(i, slot, start, size, sem, peer):
        return pltpu.make_async_remote_copy(
            src_ref=part.at[i, pl.ds(start, size)],
            dst_ref=landed.at[slot, pl.ds(start, size)],
            send_sem=tp_send.at[sem],
            recv_sem=tp_recv.at[sem],
            device_id=(ex, peer),
            device_id_type=MESH,
        )

    arrive(0)
    first = []
    for n in range(examples):
        project(0, n * SEQ, SEQ)
        copy = send(0, 0, n * SEQ, SEQ, n, near)
        copy.start()
        first.append(copy)
    arrive(1)
    across = []
    for n in range(examples):
        project(1, n * SEQ, SEQ)
        first[n].wait_recv()
        span = slice(n * SEQ, (n + 1) * SEQ)
        part[1, span] += landed[0, span]
        copy = send(1, 1, n * SEQ, SEQ, examples + n, far)
        copy.start()
        across.append(copy)
    arrive(2)
    project(2, 0, tokens)
    second = send(2, 2, 0, tokens, 2 * examples, near)
    second.start()
    arrive(3)
    project(3, 0, tokens)
    load_e.wait()
    scale = eigen_v[...] + DAMP
    second.wait_recv()
    total[...] = part[3] + landed[2]
    query_copies[1].wait_recv()
    query_copies[2].start()
    query_copies[0].wait_recv()
    query_copies[3].start()

    for n in range(examples):
        span = slice(n * SEQ, (n + 1) * SEQ)
        across[n].wait_recv()
        both = total[span] + landed[1, span]
        grad = lax.dot_general(
            both[:, KA:],
            both[:, :KA],
            (((0,), (0,)), ((), ())),
            precision=lax.Precision.HIGHEST,
            preferred_element_type=jnp.float32,
        )
        ratio[span] = (grad / SEQ) / scale
        for g in range(KG):
            at = (g * KA) % quarter
            flat[g * KA // quarter, n : n + 1, at : at + KA] = ratio[n * SEQ + g : n * SEQ + g + 1, :]
    rows[...] = flat[...].astype(jnp.bfloat16)
    row_copies = []
    for s, (h, j) in enumerate(slots):
        if s == 0:
            continue
        copy = pltpu.make_async_remote_copy(
            src_ref=rows.at[(tp + j) % 4],
            dst_ref=gathered.at[s],
            send_sem=row_send.at[s],
            recv_sem=row_recv.at[s],
            device_id=row_peer(h, j),
            device_id_type=MESH,
        )
        copy.start()
        row_copies.append(copy)
    lane = lax.broadcasted_iota(jnp.int32, (1, 4 * queries), 1)
    block = sum((lane >= m * queries).astype(jnp.int32) for m in range(1, 4))
    for copy in tables:
        copy.wait()
    codes = []
    for n in range(examples):
        codes.append([])
        for e in range(cand_ref.shape[1]):
            owner = map_ref[cand_ref[n, e]]
            low = (lo + owner) % 2 + 2 * ((lo // 2 + owner // 2) % 2)
            code = 4 * ((owner // 4 - hi + groups) % groups) + low
            codes[n].append(jnp.where(e < count_ref[n], code, -1))
    wide[0:examples, :] = rows[tp].astype(jnp.float32)
    load_q.wait()
    for copy in query_copies[2:]:
        copy.wait_recv()
    for s in range(1, len(slots)):
        row_copies[s - 1].wait_recv()
        wide[s * examples : (s + 1) * examples, :] = gathered[s].astype(jnp.float32)
    values = lax.dot_general(
        wide[...].astype(jnp.bfloat16),
        query_v[...],
        (((1,), (1,)), ((), ())),
        preferred_element_type=jnp.float32,
    )
    for s in range(len(slots)):
        scores[s] = values[s * examples : (s + 1) * examples, :]
    val_copies = []
    for s, (h, j) in enumerate(slots):
        if s == 0:
            continue
        copy = pltpu.make_async_remote_copy(
            src_ref=scores.at[s],
            dst_ref=returned.at[s],
            send_sem=val_send.at[s],
            recv_sem=val_recv.at[s],
            device_id=row_source(h, j),
            device_id_type=MESH,
        )
        copy.start()
        val_copies.append(copy)
    for copy in (*first, *across, second, *query_copies, *row_copies):
        copy.wait_send()
    for copy in val_copies:
        copy.wait_recv()
    sums = []
    for h in range(groups):
        own = scores[0] if h == 0 else returned[4 * h]
        sums.append((own + returned[4 * h + 1]) + (returned[4 * h + 2] + returned[4 * h + 3]))
    slot_total = cand_ref.shape[1]
    for n in range(examples):
        for e in range(slot_total):
            row = jnp.zeros((1, 4 * queries), jnp.float32)
            for h in range(groups):
                row += jnp.where(block + 4 * h == codes[n][e], sums[h][n : n + 1], 0.0)
            picked[n * slot_total + e : n * slot_total + e + 1, :] = row
    chosen = picked[...]
    chosen = (chosen[:, :queries] + chosen[:, queries : 2 * queries]) + (
        chosen[:, 2 * queries : 3 * queries] + chosen[:, 3 * queries :]
    )
    for n in range(examples):
        out_ref[n] = chosen[n * slot_total : (n + 1) * slot_total]
    for copy in val_copies:
        copy.wait_send()


def shards(acts, out_grads, basis_in, basis_out, eigen, query_grads, candidates, counts, owner_map):
    owners = lax.axis_size("ex")
    assert lax.axis_size("tp") == 4 and owners % 4 == 0
    groups, quarter = owners // 4, query_grads.shape[1] // 4
    examples, slot_total = candidates.shape
    tokens = examples * SEQ
    queries = query_grads.shape[0]
    vmem = pltpu.VMEM
    dma = pltpu.SemaphoreType.DMA
    return pl.pallas_call(
        functools.partial(kernel, owners, examples),
        out_shape=jax.ShapeDtypeStruct((examples, slot_total, queries), jnp.float32),
        in_specs=[pl.BlockSpec(memory_space=pl.ANY)] * 9,
        out_specs=pl.BlockSpec(memory_space=pltpu.VMEM),
        scratch_shapes=[
            vmem((4, tokens, acts.shape[1]), jnp.bfloat16),
            vmem((4, tokens, out_grads.shape[1]), jnp.bfloat16),
            vmem(basis_in.shape, jnp.bfloat16),
            vmem(basis_out.shape, jnp.bfloat16),
            vmem(eigen.shape, jnp.float32),
            vmem((4 * queries, quarter), jnp.bfloat16),
            vmem((4, tokens, KA + KG), jnp.float32),
            vmem((3, tokens, KA + KG), jnp.float32),
            vmem((tokens, KA + KG), jnp.float32),
            vmem((tokens, KA), jnp.float32),
            vmem((4, examples, quarter), jnp.float32),
            vmem((4, examples, quarter), jnp.bfloat16),
            vmem((owners, examples, quarter), jnp.bfloat16),
            vmem((owners * examples, quarter), jnp.float32),
            vmem((owners, examples, 4 * queries), jnp.float32),
            vmem((owners, examples, 4 * queries), jnp.float32),
            vmem((examples * slot_total, 4 * queries), jnp.float32),
            pltpu.SMEM(candidates.shape, jnp.int32),
            pltpu.SMEM(counts.shape, jnp.int32),
            pltpu.SMEM(owner_map.shape, jnp.int32),
            dma((15,)),
            dma((2 * examples + 1,)),
            dma((2 * examples + 1,)),
            dma((4,)),
            dma((4,)),
            dma((owners,)),
            dma((owners,)),
            dma((owners,)),
            dma((owners,)),
        ],
        compiler_params=pltpu.CompilerParams(
            collective_id=0, has_side_effects=True, vmem_limit_bytes=60 << 20
        ),
    )(acts, out_grads, basis_in, basis_out, eigen, query_grads, candidates, counts, owner_map)


def solution(mesh):
    in_specs = (
        P("ex", "tp"),
        P("ex", "tp"),
        P("tp", None),
        P("tp", None),
        P(),
        P("ex", None),
        P(("ex", "tp"), None),
        P(("ex", "tp")),
        P(),
    )
    out_specs = P(("ex", "tp"), None, None)
    return jax.shard_map(shards, mesh=mesh, in_specs=in_specs, out_specs=out_specs, check_vma=False)
```
